256 devices in a mesh: grp: 8 (over y, x_hi), shard: 32 (over z, x_lo, core).
Axes of the slice: x: 4 (x_hi: 2, x_lo: 2; x = x_hi * 2 + x_lo), y: 4, z: 8, core: 2. Of those that a mesh axis runs over, the one named last changes fastest.
Arguments:
- src: float32 [4096, 1024], P(('grp', 'shard')), may hold values from -64 to 64
- inv_src: float32 [4096], P(('grp', 'shard')), may hold values from 5 to 250
- tgt: float32 [32768, 1024], P(('shard', 'grp')), may hold values from -64 to 64
- inv_tgt: float32 [32768], P(('shard', 'grp')), may hold values from 5 to 250
Outputs:
- margin: float32 [4096, 32768], P('grp', 'shard')
The draws below stay inside these ranges and needn't reach their ends.
All inputs are finite; a program needn't handle non-finite values.
Results may differ from the reference program's by a relative error of at most 0.00013.
Values sent between devices are 32-bit elements; how exact they have to be, the bound alone decides.
No kernel may reach another device: no remote copies, remote signals or barrier semaphores. Data moves between devices by JAX's collectives and lax.ppermute only.
A program may use at most 64 MiB of HBM per device.

```python
import math
import jax
import jax.numpy as jnp
from jax import lax

D = 1024
SOURCES = 4096
TARGETS = 32768


def embeddings(key):
    keys = jax.random.split(jax.random.fold_in(key, 11), 2)
    src = jax.random.normal(keys[0], (SOURCES, D), jnp.float32)
    tgt = jax.random.normal(keys[1], (TARGETS, D), jnp.float32)
    return (jnp.clip(src, -64.0, 64.0), jnp.clip(tgt, -64.0, 64.0))


def draw_src(key, part):
    return embeddings(key)[0]


def draw_tgt(key, part):
    return embeddings(key)[1]


def draw_inv_src(key, part):
    rates = jnp.exp(jax.random.uniform(jax.random.fold_in(key, 21), (SOURCES,), jnp.float32, math.log(5.0), math.log(100.0)))
    return rates


def draw_inv_tgt(key, part):
    rates = jnp.exp(jax.random.uniform(jax.random.fold_in(key, 31), (TARGETS,), jnp.float32, math.log(5.0), math.log(100.0)))
    return rates


def setup_inputs(seed: int = 0) -> dict:
    arg_keys = jax.random.split(jax.random.key(seed), 5)
    src = draw_src(jax.random.fold_in(arg_keys[4], 71), 0)
    inv_src = draw_inv_src(jax.random.fold_in(arg_keys[4], 71), 0)
    tgt = draw_tgt(jax.random.fold_in(arg_keys[4], 71), 0)
    inv_tgt = draw_inv_tgt(jax.random.fold_in(arg_keys[4], 71), 0)
    return dict(src=src, inv_src=inv_src, tgt=tgt, inv_tgt=inv_tgt)


def unit_rows(rows):
    return rows * lax.rsqrt(lax.optimization_barrier(jnp.sum(rows * rows, axis=1, keepdims=True)) + 1e-06)

def reference(src, inv_src, tgt, inv_tgt):
    src_unit = unit_rows(src)
    tgt_unit = unit_rows(tgt)
    sims = jnp.dot(src_unit, tgt_unit.T, precision=lax.Precision.HIGHEST, preferred_element_type=jnp.float32)
    row_lse = jax.nn.logsumexp(sims * inv_src[:, None], axis=1) - math.log(TARGETS)
    col_lse = jax.nn.logsumexp(sims * inv_tgt[None, :], axis=0) - math.log(SOURCES)
    scale = 0.5 * (inv_src[:, None] + inv_tgt[None, :])
    return sims * scale - (jnp.logaddexp(row_lse[:, None], col_lse[None, :]) - math.log(2.0))
```

```python
import functools
import math

import jax
import jax.numpy as jnp
from jax import lax
from jax.experimental import pallas as pl
from jax.experimental.pallas import tpu as pltpu
from jax.sharding import Mesh
from jax.sharding import PartitionSpec as P


FINE = ("y", "xh", "z", "xl", "c")
SRC = ("y", "xh", "z", "xl", "c")
TGT = ("z", "xl", "c", "y", "xh")
LANES = 128
NT = (((1,), (1,)), ((), ()))


def shifted(value, axis, by):
    n = lax.axis_size(axis)
    return lax.ppermute(value, axis, [(i, (i + by) % n) for i in range(n)])


def rows_kernel(*refs):
    *groups, hi_ref, lo_ref, inv_ref = refs
    z, xl, c = lax.axis_index("z"), lax.axis_index("xl"), lax.axis_index("c")
    for (zs, dc), ref in zip(ROW_GROUPS, groups):
        at = 0
        for dz in zs:
            for dx in (0, 1):
                block = ref[at]
                at += 1
                place = lax.rem(z + dz + 8, 8) * 64 + (xl ^ dx) * 32 + (c ^ dc) * 16
                place = pl.multiple_of(place, 16)
                tiles = block[:128].reshape(2, 8, 8, LANES)
                square = jnp.sum(tiles * tiles, axis=1)
                total = jnp.sum(square, axis=-1, keepdims=True)
                scale = jnp.broadcast_to(lax.rsqrt(total + 1e-06), square.shape)
                for k in range(8):
                    unit = (tiles[:, k] * scale).reshape(16, LANES)
                    hi = unit.astype(jnp.bfloat16)
                    lo = (unit - hi.astype(jnp.float32)).astype(jnp.bfloat16)
                    hi_ref[pl.ds(place, 16), k * LANES : (k + 1) * LANES] = hi
                    lo_ref[pl.ds(place, 16), k * LANES : (k + 1) * LANES] = lo
                inv_ref[pl.ds(place, 16), :] = block[128:]


EVEN, DOWN, UP = (0, -2, 2, 4), (-1, -3), (1, 3)
ROW_GROUPS = tuple((zs, dc) for dc in (0, 1) for zs in (EVEN, DOWN, UP))


def rows_ready(groups):
    whole = pl.BlockSpec(memory_space=pltpu.VMEM)
    return pl.pallas_call(
        rows_kernel,
        out_shape=(
            jax.ShapeDtypeStruct((512, 1024), jnp.bfloat16),
            jax.ShapeDtypeStruct((512, 1024), jnp.bfloat16),
            jax.ShapeDtypeStruct((512, LANES), jnp.float32),
        ),
        in_specs=[whole] * len(groups),
        out_specs=(whole,) * 3,
        compiler_params=pltpu.CompilerParams(vmem_limit_bytes=16 << 20),
        cost_estimate=pl.CostEstimate(flops=8 << 20, bytes_accessed=5 << 20, transcendentals=0),
    )(*groups)


def to_lanes(column):
    same = lax.broadcasted_iota(jnp.int32, (LANES, LANES), 0) == lax.broadcasted_iota(
        jnp.int32, (LANES, LANES), 1
    )
    wide = jnp.broadcast_to(column, (512, LANES)).reshape(4, LANES, LANES)
    return jnp.sum(jnp.where(same[None], wide, 0.0), axis=1)


def from_lanes(lines):
    same = lax.broadcasted_iota(jnp.int32, (LANES, LANES), 0) == lax.broadcasted_iota(
        jnp.int32, (LANES, LANES), 1
    )
    wide = jnp.broadcast_to(lines[:, None, :], (4, LANES, LANES))
    return jnp.sum(jnp.where(same[None], wide, 0.0), axis=2).reshape(512, 1)


def tile_kernel(layout, last, *refs):
    n = sum(len(parts) for parts in layout)
    pieces, refs = refs[:n], refs[n:]
    hi_ref, lo_ref, inv_ref, tinv_ref = refs[:4]
    refs = refs[4:]
    if last:
        before_ref, refs = refs[0], refs[1:]
    sims_ref, col_ref, row_ref, bhi, blo = refs
    y = lax.axis_index("y")
    k = 0
    for dy, parts in zip((0, -1, 1, 2), layout):
        place = pl.multiple_of(lax.rem(y + dy + 4, 4) * LANES, LANES)
        at = 0
        for rows in parts:
            value = pieces[k][:rows]
            k += 1
            total = jnp.sum(value * value, axis=1, keepdims=True)
            unit = value * lax.rsqrt(total + 1e-06)
            hi = unit.astype(jnp.bfloat16)
            bhi[pl.ds(pl.multiple_of(place + at, 16), rows), :] = hi
            blo[pl.ds(pl.multiple_of(place + at, 16), rows), :] = (
                unit - hi.astype(jnp.float32)
            ).astype(jnp.bfloat16)
            at += rows
    dot = functools.partial(lax.dot_general, preferred_element_type=jnp.float32)
    sims = dot(hi_ref[...], bhi[...], NT)
    sims += dot(hi_ref[...], blo[...], NT)
    sims += dot(lo_ref[...], bhi[...], NT)
    sims_ref[...] = sims
    inv = inv_ref[:, :1]
    logits = sims * inv
    top = jnp.max(logits, axis=1, keepdims=True)
    total = jnp.sum(jnp.exp(logits - top), axis=1, keepdims=True)
    lines_top, lines_total = to_lanes(top), to_lanes(total)
    if last:
        other_top, other_total = before_ref[0:4, :], before_ref[4:8, :]
        best = jnp.maximum(lines_top, other_top)
        lines_total = lines_total * jnp.exp(lines_top - best) + other_total * jnp.exp(other_top - best)
        lines_top = best
    row_ref[0:4, :] = lines_top
    row_ref[4:8, :] = lines_total
    for j in range(4):
        logits = sims[:, j * LANES : (j + 1) * LANES] * tinv_ref[j : j + 1, :]
        top = jnp.max(logits, axis=0, keepdims=True)
        col_ref[j : j + 1, :] = top
        col_ref[4 + j : 5 + j, :] = jnp.sum(jnp.exp(logits - top), axis=0, keepdims=True)


def tile(layout, pieces, hi, lo, inv, tinv, before=None):
    whole = pl.BlockSpec(memory_space=pltpu.VMEM)
    last = before is not None
    operands = (*pieces, hi, lo, inv, tinv, *((before,) if last else ()))
    return pl.pallas_call(
        functools.partial(tile_kernel, layout, last),
        out_shape=(
            jax.ShapeDtypeStruct((512, 512), jnp.float32),
            jax.ShapeDtypeStruct((8, LANES), jnp.float32),
            jax.ShapeDtypeStruct((8, LANES), jnp.float32),
        ),
        in_specs=[whole] * len(operands),
        out_specs=(whole,) * 3,
        scratch_shapes=[pltpu.VMEM((512, 1024), jnp.bfloat16)] * 2,
        compiler_params=pltpu.CompilerParams(vmem_limit_bytes=24 << 20),
        cost_estimate=pl.CostEstimate(
            flops=3 << 29, bytes_accessed=6 << 20, transcendentals=1 << 19
        ),
    )(*operands)


def final_kernel(same_ref, other_ref, inv_ref, tsame_ref, tother_ref, row_ref, col_ref, out_ref):
    xh = lax.axis_index("xh")
    row = from_lanes(row_ref[0:4, :] + jnp.log(row_ref[4:8, :])) - math.log(32768)
    inv = inv_ref[:, :1]
    col = col_ref[0:8, :] + jnp.log(col_ref[8:16, :]) - math.log(4096)
    for side, (sims_ref, tinv_ref) in enumerate(((same_ref, tsame_ref), (other_ref, tother_ref))):
        for j in range(4):
            place = pl.multiple_of((2 * j + (xh ^ side)) * LANES, LANES)
            right = col[4 * side + j : 4 * side + j + 1, :]
            top = jnp.maximum(row, right)
            gap = jnp.minimum(row, right) - top
            both = top + jnp.log(1.0 + jnp.exp(gap)) - math.log(2.0)
            scale = 0.5 * (inv + tinv_ref[j : j + 1, :])
            sims = sims_ref[:, j * LANES : (j + 1) * LANES]
            out_ref[:, pl.ds(place, LANES)] = sims * scale - both


def final(same, other, inv, tsame, tother, row, col):
    whole = pl.BlockSpec(memory_space=pltpu.VMEM)
    return pl.pallas_call(
        final_kernel,
        out_shape=jax.ShapeDtypeStruct((512, 1024), jnp.float32),
        in_specs=[whole] * 7,
        out_specs=whole,
        compiler_params=pltpu.CompilerParams(vmem_limit_bytes=24 << 20),
    )(same, other, inv, tsame, tother, row, col)


def joined(values):
    half = values[0].shape[0] // 2
    best = functools.reduce(jnp.maximum, [v[:half] for v in values])
    total = sum(v[half:] * jnp.exp(v[:half] - best) for v in values)
    return jnp.concatenate([best, total])


def gathered_rows(src, inv_src):
    tiles = src.reshape(2, 8, 8, LANES).transpose(0, 2, 1, 3).reshape(128, LANES)
    own = jnp.concatenate([tiles, jnp.broadcast_to(inv_src[:, None], (16, LANES))])
    pair = jnp.stack([own, shifted(own, "xl", 1)])
    below, above, across = (shifted(pair, "z", k) for k in (2, -2, 4))
    even = jnp.concatenate([pair, below, above, across])
    down = shifted(even[:4], "z", 1)
    up = shifted(jnp.concatenate([pair, above]), "z", -1)
    odd = shifted(jnp.concatenate([down, up]), "c", 1)
    twin = shifted(even, "c", 1)
    return even, down, up, twin, odd[:4], odd[4:]


CUT = 48


def gathered_columns(tgt, inv_tgt):
    line = jnp.pad(inv_tgt[None, :], ((0, 7), (0, 1024 - LANES)))
    down = shifted(tgt, "y", 1)
    up = shifted(tgt, "y", -1)
    q = shifted(jnp.concatenate([tgt[CUT:], line]), "xh", 1)
    q_own = shifted(tgt[:CUT], "xh", 1)
    rows = LANES - CUT
    head = jnp.concatenate([q[rows : rows + 1], jnp.pad(inv_tgt[None, :], ((0, 6), (0, 1024 - LANES)))])
    q = jnp.concatenate([q[:rows], head])
    q_down = shifted(q, "y", 1)
    q_up = shifted(q, "y", -1)
    far_a = shifted(down[:64], "y", 1)
    far_b = shifted(up[64:], "y", -1)
    q_d = shifted(down[:CUT], "xh", 1)
    q_u = shifted(up[:CUT], "xh", 1)
    half = rows // 2
    q_far_a = shifted(q_down[:half], "y", 1)
    q_far_b = shifted(q_up[half:], "y", -1)
    q_f = shifted(far_a[:CUT], "xh", 1)
    same = ((LANES,), (LANES,), (LANES,), (64, 64)), (tgt, down, up, far_a, far_b)
    other = (
        ((CUT, rows), (CUT, rows), (CUT, rows), (CUT, half, half)),
        (q_own, q, q_d, q_down, q_u, q_up, q_f, q_far_a, q_far_b),
    )
    y = lax.axis_index("y")

    tails = (q[rows:], q_down[rows:], q_up[rows:], q_far_b[half:])
    t_same = jnp.concatenate([t[1:2, :LANES] for t in tails])
    t_other = jnp.concatenate([t[0:1, :LANES] for t in tails])
    def by_y(t):
        t = jnp.stack([t[0], t[2], t[3], t[1]])
        return jnp.select([y == k for k in range(4)], [jnp.roll(t, k, axis=0) for k in range(4)])

    return same, other, by_y(t_same), by_y(t_other)


def body(src, inv_src, tgt, inv_tgt):
    same, other, t_same, t_other = gathered_columns(tgt, inv_tgt)
    hi, lo, inv = rows_ready(gathered_rows(src, inv_src))
    sims_same, col_same, row = tile(*same, hi, lo, inv, t_same)
    sims_other, col_other, row = tile(*other, hi, lo, inv, t_other, row)
    col = jnp.concatenate([col_same[:4], col_other[:4], col_same[4:], col_other[4:]])
    col = joined([col] + [shifted(col, "y", k) for k in (1, -1, 2)])
    over = shifted(col, "xh", 1)
    over = jnp.concatenate([over[4:8], over[0:4], over[12:16], over[8:12]])
    row = joined([row, shifted(row, "c", 1)])
    row = joined([row] + [shifted(row, "z", k) for k in (2, -2, 4)])
    flip = [(i, i ^ 1) for i in range(8)]
    turned = lax.ppermute(row, "z", flip)
    crossed = lax.ppermute(
        row, ("z", "xl"), [(2 * i + k, 2 * (i ^ 1) + (k ^ 1)) for i in range(8) for k in range(2)]
    )
    row = joined([row, turned, shifted(row, "xl", 1), crossed])
    col = joined([col, over])
    return final(sims_same, sims_other, inv, t_same, t_other, row, col)


def solution(mesh):
    finer = Mesh(mesh.devices.reshape(4, 2, 8, 2, 2), FINE)
    placed = (P(SRC, None), P(SRC), P(TGT, None), P(TGT))
    return jax.shard_map(
        body,
        mesh=finer,
        in_specs=placed,
        out_specs=P(("y", "xh"), ("z", "xl", "c")),
        check_vma=False,
    )
```

```python
import functools
import math

import jax
import jax.numpy as jnp
from jax import lax
from jax.experimental import pallas as pl
from jax.experimental.pallas import tpu as pltpu
from jax.sharding import Mesh
from jax.sharding import PartitionSpec as P


FINE = ("y", "xh", "z", "xl", "c")
SRC = ("y", "xh", "z", "xl", "c")
TGT = ("z", "xl", "c", "y", "xh")
LANES = 128
NT = (((1,), (1,)), ((), ()))


CUT = 48
REST = LANES - CUT


def shifted(value, axis, by):
    n = lax.axis_size(axis)
    return lax.ppermute(value, axis, [(i, (i + by) % n) for i in range(n)])


def whole():
    return pl.BlockSpec(memory_space=pltpu.VMEM)


def first_kernel(src_ref, inv_ref, tgt_ref, tinv_ref, own_ref, q_ref, p_ref, rows, lane, tlane, sems):
    pairs = (
        (tgt_ref.at[CUT:], q_ref.at[:REST]),
        (tgt_ref.at[:CUT], p_ref),
        (src_ref, rows),
        (inv_ref, lane),
        (tinv_ref, tlane),
    )
    copies = [pltpu.make_async_copy(a, b, sems.at[k]) for k, (a, b) in enumerate(pairs)]
    for copy in copies:
        copy.start()
    q_ref[REST:, :] = jnp.zeros((8, 1024), jnp.float32)
    for copy in copies[2:]:
        copy.wait()
    for k in range(8):
        for r in range(2):
            at = r * 64 + k * 8
            own_ref[at : at + 8, :] = rows[r * 8 : r * 8 + 8, k * LANES : (k + 1) * LANES]
    same = lax.broadcasted_iota(jnp.int32, (16, 16), 0) == lax.broadcasted_iota(
        jnp.int32, (16, 16), 1
    )
    wide = jnp.where(same, jnp.broadcast_to(lane[...], (16, 16)), 0.0)
    own_ref[128:144, :] = jnp.broadcast_to(jnp.sum(wide, axis=1, keepdims=True), (16, LANES))
    q_ref[REST : REST + 1, :LANES] = tlane[...]
    for copy in copies[:2]:
        copy.wait()


def first_blocks(src, inv_src, tgt, inv_tgt):
    return pl.pallas_call(
        first_kernel,
        out_shape=(
            jax.ShapeDtypeStruct((144, LANES), jnp.float32),
            jax.ShapeDtypeStruct((REST + 8, 1024), jnp.float32),
            jax.ShapeDtypeStruct((CUT, 1024), jnp.float32),
        ),
        in_specs=[pl.BlockSpec(memory_space=pl.ANY)] * 4,
        out_specs=(whole(),) * 3,
        scratch_shapes=[
            pltpu.VMEM((16, 1024), jnp.float32),
            pltpu.VMEM((1, 16), jnp.float32),
            pltpu.VMEM((1, LANES), jnp.float32),
            pltpu.SemaphoreType.DMA((5,)),
        ],
        compiler_params=pltpu.CompilerParams(vmem_limit_bytes=60 << 20),
        cost_estimate=pl.CostEstimate(flops=1 << 16, bytes_accessed=1 << 20, transcendentals=0),
    )(src, inv_src[None, :], tgt, inv_tgt[None, :])


def rows_kernel(*refs):
    *groups, hi_ref, lo_ref, inv_ref = refs
    z, xl, c = lax.axis_index("z"), lax.axis_index("xl"), lax.axis_index("c")
    for (zs, dc), ref in zip(ROW_GROUPS, groups):
        at = 0
        for dz in zs:
            for dx in (0, 1):
                block = ref[at]
                at += 1
                place = lax.rem(z + dz + 8, 8) * 64 + (xl ^ dx) * 32 + (c ^ dc) * 16
                place = pl.multiple_of(place, 16)
                tiles = block[:128].reshape(2, 8, 8, LANES)
                square = jnp.sum(tiles * tiles, axis=1)
                total = jnp.sum(square, axis=-1, keepdims=True)
                scale = jnp.broadcast_to(lax.rsqrt(total + 1e-06), square.shape)
                for k in range(8):
                    unit = (tiles[:, k] * scale).reshape(16, LANES)
                    hi = unit.astype(jnp.bfloat16)
                    lo = (unit - hi.astype(jnp.float32)).astype(jnp.bfloat16)
                    hi_ref[pl.ds(place, 16), k * LANES : (k + 1) * LANES] = hi
                    lo_ref[pl.ds(place, 16), k * LANES : (k + 1) * LANES] = lo
                inv_ref[pl.ds(place, 16), :] = block[128:]


ROW_GROUPS = tuple((zs, dc) for dc in (0, 1) for zs in ((0, -2, 2, 4), (-1, -3, 1, 3)))


def rows_ready(groups):
    return pl.pallas_call(
        rows_kernel,
        out_shape=(
            jax.ShapeDtypeStruct((512, 1024), jnp.bfloat16),
            jax.ShapeDtypeStruct((512, 1024), jnp.bfloat16),
            jax.ShapeDtypeStruct((512, LANES), jnp.float32),
        ),
        in_specs=[whole()] * len(groups),
        out_specs=(whole(),) * 3,
        compiler_params=pltpu.CompilerParams(vmem_limit_bytes=16 << 20),
        cost_estimate=pl.CostEstimate(flops=8 << 20, bytes_accessed=5 << 20, transcendentals=0),
    )(*groups)


def to_lanes(column):
    same = lax.broadcasted_iota(jnp.int32, (LANES, LANES), 0) == lax.broadcasted_iota(
        jnp.int32, (LANES, LANES), 1
    )
    wide = jnp.broadcast_to(column, (512, LANES)).reshape(4, LANES, LANES)
    return jnp.sum(jnp.where(same[None], wide, 0.0), axis=1)


def from_lanes(lines):
    same = lax.broadcasted_iota(jnp.int32, (LANES, LANES), 0) == lax.broadcasted_iota(
        jnp.int32, (LANES, LANES), 1
    )
    wide = jnp.broadcast_to(lines[:, None, :], (4, LANES, LANES))
    return jnp.sum(jnp.where(same[None], wide, 0.0), axis=2).reshape(512, 1)


LAYOUTS = (((LANES,),) * 4, ((CUT, REST),) * 4)


def tile_kernel(side, *refs):
    n = sum(len(parts) for parts in LAYOUTS[side])
    pieces, refs = refs[:n], refs[n:]
    hi_ref, lo_ref, inv_ref, *refs = refs
    y = lax.axis_index("y")
    if side == 1:
        before_ref, before_sims, *refs = refs
        tails, refs = refs[:4], refs[4:]
        sims_ref, row_ref, col_ref, tinv_ref, bhi, blo = refs
        for dy, tail in zip((0, -1, 1, 2), tails):
            spot = lax.rem(y + dy + 4, 4)
            tinv_ref[pl.ds(spot, 1), :] = tail[1:2, :]
            tinv_ref[pl.ds(spot + 4, 1), :] = tail[0:1, :]
    else:
        sims_ref, row_ref, bhi, blo = refs
    k = 0
    for dy, parts in zip((0, -1, 1, 2), LAYOUTS[side]):
        spot = lax.rem(y + dy + 4, 4)
        at = 0
        for rows in parts:
            value = pieces[k][:rows, :]
            k += 1
            total = jnp.sum(value * value, axis=1, keepdims=True)
            unit = value * lax.rsqrt(total + 1e-06)
            hi = unit.astype(jnp.bfloat16)
            place = pl.ds(pl.multiple_of(spot * LANES + at, 8), rows)
            bhi[place, :] = hi
            blo[place, :] = (unit - hi.astype(jnp.float32)).astype(jnp.bfloat16)
            at += rows
    dot = functools.partial(lax.dot_general, preferred_element_type=jnp.float32)
    sims = dot(hi_ref[...], bhi[...], NT)
    sims += dot(hi_ref[...], blo[...], NT)
    sims += dot(lo_ref[...], bhi[...], NT)
    sims_ref[...] = sims
    inv = inv_ref[:, :1]
    logits = sims * inv
    top = jnp.max(logits, axis=1, keepdims=True)
    total = jnp.sum(jnp.exp(logits - top), axis=1, keepdims=True)
    lines_top, lines_total = to_lanes(top), to_lanes(total)
    if side == 1:
        other_top, other_total = before_ref[0:4, :], before_ref[4:8, :]
        best = jnp.maximum(lines_top, other_top)
        lines_total = lines_total * jnp.exp(lines_top - best) + other_total * jnp.exp(other_top - best)
        lines_top = best
    row_ref[0:4, :] = lines_top
    row_ref[4:8, :] = lines_total
    if side == 1:
        for j in range(8):
            k = (j % 4) * LANES
            part = before_sims[:, k : k + LANES] if j < 4 else sims[:, k : k + LANES]
            logits = part * tinv_ref[j : j + 1, :]
            top = jnp.max(logits, axis=0, keepdims=True)
            col_ref[j : j + 1, :] = top
            col_ref[8 + j : 9 + j, :] = jnp.sum(jnp.exp(logits - top), axis=0, keepdims=True)


def tile(side, pieces, *operands):
    operands = (*pieces, *operands)
    shapes = [
        jax.ShapeDtypeStruct((512, 512), jnp.float32),
        jax.ShapeDtypeStruct((8, LANES), jnp.float32),
    ]
    if side == 1:
        shapes += [
            jax.ShapeDtypeStruct((16, LANES), jnp.float32),
            jax.ShapeDtypeStruct((8, LANES), jnp.float32),
        ]
    return pl.pallas_call(
        functools.partial(tile_kernel, side),
        out_shape=shapes,
        in_specs=[whole()] * len(operands),
        out_specs=[whole()] * len(shapes),
        scratch_shapes=[pltpu.VMEM((512, 1024), jnp.bfloat16)] * 2,
        compiler_params=pltpu.CompilerParams(vmem_limit_bytes=24 << 20),
        cost_estimate=pl.CostEstimate(
            flops=3 << 29, bytes_accessed=6 << 20, transcendentals=1 << 19
        ),
    )(*operands)


def final_kernel(same_ref, other_ref, inv_ref, tinv_ref, row_ref, col_ref, out_ref):
    xh = lax.axis_index("xh")
    row = from_lanes(row_ref[0:4, :] + jnp.log(row_ref[4:8, :])) - math.log(32768)
    inv = inv_ref[:, :1]
    col = col_ref[0:8, :] + jnp.log(col_ref[8:16, :]) - math.log(4096)
    for side, sims_ref in enumerate((same_ref, other_ref)):
        for j in range(4):
            place = pl.multiple_of((2 * j + (xh ^ side)) * LANES, LANES)
            right = col[4 * side + j : 4 * side + j + 1, :]
            top = jnp.maximum(row, right)
            gap = jnp.minimum(row, right) - top
            both = top + jnp.log(1.0 + jnp.exp(gap)) - math.log(2.0)
            scale = 0.5 * (inv + tinv_ref[4 * side + j : 4 * side + j + 1, :])
            sims = sims_ref[:, j * LANES : (j + 1) * LANES]
            out_ref[:, pl.ds(place, LANES)] = sims * scale - both


def final(*operands):
    return pl.pallas_call(
        final_kernel,
        out_shape=jax.ShapeDtypeStruct((512, 1024), jnp.float32),
        in_specs=[whole()] * 6,
        out_specs=whole(),
        compiler_params=pltpu.CompilerParams(vmem_limit_bytes=24 << 20),
    )(*operands)


def joined(values):
    half = values[0].shape[0] // 2
    best = functools.reduce(jnp.maximum, [v[:half] for v in values])
    total = sum(v[half:] * jnp.exp(v[:half] - best) for v in values)
    return jnp.concatenate([best, total])


def gathered_rows(own):
    pair = jnp.stack([own, shifted(own, "xl", 1)])
    below = shifted(pair, "z", 2)
    above = shifted(pair, "z", -2)
    across = shifted(pair, "z", 4)
    down = shifted(jnp.concatenate([pair, below]), "z", 1)
    up = shifted(jnp.concatenate([pair, above]), "z", -1)
    near = jnp.concatenate([pair, below, above, across])
    rest = jnp.concatenate([down, up])
    return near, rest, shifted(near, "c", 1), shifted(rest, "c", 1)


def gathered_columns(tgt, inv_tgt, q, p):
    down = shifted(tgt, "y", 1)
    up = shifted(tgt, "y", -1)
    far = shifted(tgt, "y", 2)
    q = shifted(q, "xh", 1)
    q_own = shifted(p, "xh", 1)
    tail = [inv_tgt[None, :], jnp.zeros((6, LANES), jnp.float32)]
    tail = jnp.pad(jnp.concatenate(tail), ((0, 0), (0, 1024 - LANES)))
    q = jnp.concatenate([q[: REST + 1], tail])
    q_down = shifted(q, "y", 1)
    q_up = shifted(q, "y", -1)
    q_far = shifted(q, "y", 2)
    both = jnp.concatenate([down[:CUT], up[:CUT]])
    q_both = shifted(both, "xh", 1)
    q_f = shifted(far[:CUT], "xh", 1)
    same = (tgt, down, up, far)
    other = (q_own, q, q_both[:CUT], q_down, q_both[CUT:], q_up, q_f, q_far)
    return same, other, tuple(v[REST : REST + 2, :LANES] for v in (q, q_down, q_up, q_far))


def all_rows(row):
    row = joined([row, shifted(row, "c", 1)])
    row = joined([row] + [shifted(row, "z", k) for k in (2, -2, 4)])
    flip = [(i, i ^ 1) for i in range(8)]
    beside = lax.ppermute(row, "z", flip)
    crossed = lax.ppermute(
        row, ("z", "xl"), [(2 * i + k, 2 * (i ^ 1) + (k ^ 1)) for i in range(8) for k in range(2)]
    )
    return joined([row, beside, shifted(row, "xl", 1), crossed])


def all_columns(col):
    col = joined([col] + [shifted(col, "y", k) for k in (1, -1, 2)])
    over = shifted(col, "xh", 1)
    return joined([col, jnp.concatenate([over[4:8], over[0:4], over[12:16], over[8:12]])])


def body(src, inv_src, tgt, inv_tgt):
    own, q, p = first_blocks(src, inv_src, tgt, inv_tgt)
    same, other, tails = gathered_columns(tgt, inv_tgt, q, p)
    blocks = gathered_rows(own)
    hi, lo, inv = rows_ready(blocks)
    sims_same, row = tile(0, same, hi, lo, inv)
    sims_other, row, col, tinv = tile(1, other, hi, lo, inv, row, sims_same, *tails)
    col = all_columns(col)
    row = all_rows(row)
    return final(sims_same, sims_other, inv, tinv, row, col)


def solution(mesh):
    finer = Mesh(mesh.devices.reshape(4, 2, 8, 2, 2), FINE)
    placed = (P(SRC, None), P(SRC), P(TGT, None), P(TGT))
    return jax.shard_map(
        body,
        mesh=finer,
        in_specs=placed,
        out_specs=P(("y", "xh"), ("z", "xl", "c")),
        check_vma=False,
    )
```

```python
import functools
import math

import jax
import jax.numpy as jnp
from jax import lax
from jax.experimental import pallas as pl
from jax.experimental.pallas import tpu as pltpu
from jax.sharding import Mesh
from jax.sharding import PartitionSpec as P


FINE = ("y", "xh", "z", "xl", "c")
SRC = ("y", "xh", "z", "xl", "c")
TGT = ("z", "xl", "c", "y", "xh")
LANES = 128
NT = (((1,), (1,)), ((), ()))


CUT = 48
REST = LANES - CUT


def shifted(value, axis, by):
    n = lax.axis_size(axis)
    return lax.ppermute(value, axis, [(i, (i + by) % n) for i in range(n)])


def whole():
    return pl.BlockSpec(memory_space=pltpu.VMEM)


def first_kernel(src_ref, inv_ref, tgt_ref, tinv_ref, own_ref, q_ref, p_ref, rows, lane, tlane, sems):
    pairs = (
        (tgt_ref.at[CUT:], q_ref.at[:REST]),
        (tgt_ref.at[:CUT], p_ref),
        (src_ref, rows),
        (inv_ref, lane),
        (tinv_ref, tlane),
    )
    copies = [pltpu.make_async_copy(a, b, sems.at[k]) for k, (a, b) in enumerate(pairs)]
    for copy in copies:
        copy.start()
    q_ref[REST:, :] = jnp.zeros((8, 1024), jnp.float32)
    for copy in copies[2:]:
        copy.wait()
    for k in range(8):
        for r in range(2):
            at = r * 64 + k * 8
            own_ref[at : at + 8, :] = rows[r * 8 : r * 8 + 8, k * LANES : (k + 1) * LANES]
    same = lax.broadcasted_iota(jnp.int32, (16, 16), 0) == lax.broadcasted_iota(
        jnp.int32, (16, 16), 1
    )
    wide = jnp.where(same, jnp.broadcast_to(lane[...], (16, 16)), 0.0)
    own_ref[128:144, :] = jnp.broadcast_to(jnp.sum(wide, axis=1, keepdims=True), (16, LANES))
    q_ref[REST : REST + 1, :LANES] = tlane[...]
    for copy in copies[:2]:
        copy.wait()


def first_blocks(src, inv_src, tgt, inv_tgt):
    return pl.pallas_call(
        first_kernel,
        out_shape=(
            jax.ShapeDtypeStruct((144, LANES), jnp.float32),
            jax.ShapeDtypeStruct((REST + 8, 1024), jnp.float32),
            jax.ShapeDtypeStruct((CUT, 1024), jnp.float32),
        ),
        in_specs=[pl.BlockSpec(memory_space=pl.ANY)] * 4,
        out_specs=(whole(),) * 3,
        scratch_shapes=[
            pltpu.VMEM((16, 1024), jnp.float32),
            pltpu.VMEM((1, 16), jnp.float32),
            pltpu.VMEM((1, LANES), jnp.float32),
            pltpu.SemaphoreType.DMA((5,)),
        ],
        compiler_params=pltpu.CompilerParams(vmem_limit_bytes=60 << 20),
        cost_estimate=pl.CostEstimate(flops=1 << 16, bytes_accessed=1 << 20, transcendentals=0),
    )(src, inv_src[None, :], tgt, inv_tgt[None, :])


def rows_kernel(*refs):
    *groups, hi_ref, lo_ref, inv_ref = refs
    z, xl, c = lax.axis_index("z"), lax.axis_index("xl"), lax.axis_index("c")
    for (zs, dc), ref in zip(ROW_GROUPS, groups):
        at = 0
        for dz in zs:
            for dx in (0, 1):
                block = ref[at]
                at += 1
                place = lax.rem(z + dz + 8, 8) * 64 + (xl ^ dx) * 32 + (c ^ dc) * 16
                place = pl.multiple_of(place, 16)
                tiles = block[:128].reshape(2, 8, 8, LANES)
                square = jnp.sum(tiles * tiles, axis=1)
                total = jnp.sum(square, axis=-1, keepdims=True)
                scale = jnp.broadcast_to(lax.rsqrt(total + 1e-06), square.shape)
                for k in range(8):
                    unit = (tiles[:, k] * scale).reshape(16, LANES)
                    hi = unit.astype(jnp.bfloat16)
                    lo = (unit - hi.astype(jnp.float32)).astype(jnp.bfloat16)
                    hi_ref[pl.ds(place, 16), k * LANES : (k + 1) * LANES] = hi
                    lo_ref[pl.ds(place, 16), k * LANES : (k + 1) * LANES] = lo
                inv_ref[pl.ds(place, 16), :] = block[128:]


ROW_GROUPS = tuple((zs, dc) for dc in (0, 1) for zs in ((0, -2, 2, 4), (-1, -3, 1, 3)))


def rows_ready(groups):
    return pl.pallas_call(
        rows_kernel,
        out_shape=(
            jax.ShapeDtypeStruct((512, 1024), jnp.bfloat16),
            jax.ShapeDtypeStruct((512, 1024), jnp.bfloat16),
            jax.ShapeDtypeStruct((512, LANES), jnp.float32),
        ),
        in_specs=[whole()] * len(groups),
        out_specs=(whole(),) * 3,
        compiler_params=pltpu.CompilerParams(vmem_limit_bytes=16 << 20),
        cost_estimate=pl.CostEstimate(flops=8 << 20, bytes_accessed=5 << 20, transcendentals=0),
    )(*groups)


def to_lanes(column):
    same = lax.broadcasted_iota(jnp.int32, (LANES, LANES), 0) == lax.broadcasted_iota(
        jnp.int32, (LANES, LANES), 1
    )
    wide = jnp.broadcast_to(column, (512, LANES)).reshape(4, LANES, LANES)
    return jnp.sum(jnp.where(same[None], wide, 0.0), axis=1)


def from_lanes(lines):
    same = lax.broadcasted_iota(jnp.int32, (LANES, LANES), 0) == lax.broadcasted_iota(
        jnp.int32, (LANES, LANES), 1
    )
    wide = jnp.broadcast_to(lines[:, None, :], (4, LANES, LANES))
    return jnp.sum(jnp.where(same[None], wide, 0.0), axis=2).reshape(512, 1)


LAYOUTS = (((LANES,),) * 4, ((CUT, REST),) * 4)


def tile_kernel(side, *refs):
    n = sum(len(parts) for parts in LAYOUTS[side])
    pieces, refs = refs[:n], refs[n:]
    hi_ref, lo_ref, inv_ref, *refs = refs
    y = lax.axis_index("y")
    if side == 1:
        before_ref, before_sims, *refs = refs
        tails, refs = refs[:4], refs[4:]
        sims_ref, row_ref, col_ref, tinv_ref, bhi, blo = refs
        for dy, tail in zip((0, -1, 1, 2), tails):
            spot = lax.rem(y + dy + 4, 4)
            tinv_ref[pl.ds(spot, 1), :] = tail[1:2, :]
            tinv_ref[pl.ds(spot + 4, 1), :] = tail[0:1, :]
    else:
        sims_ref, row_ref, bhi, blo = refs
    k = 0
    for dy, parts in zip((0, -1, 1, 2), LAYOUTS[side]):
        spot = lax.rem(y + dy + 4, 4)
        at = 0
        for rows in parts:
            value = pieces[k][:rows, :]
            k += 1
            total = jnp.sum(value * value, axis=1, keepdims=True)
            unit = value * lax.rsqrt(total + 1e-06)
            hi = unit.astype(jnp.bfloat16)
            place = pl.ds(pl.multiple_of(spot * LANES + at, 8), rows)
            bhi[place, :] = hi
            blo[place, :] = (unit - hi.astype(jnp.float32)).astype(jnp.bfloat16)
            at += rows
    dot = functools.partial(lax.dot_general, preferred_element_type=jnp.float32)
    sims = dot(hi_ref[...], bhi[...], NT)
    sims += dot(hi_ref[...], blo[...], NT)
    sims += dot(lo_ref[...], bhi[...], NT)
    sims_ref[...] = sims
    inv = inv_ref[:, :1]
    logits = sims * inv
    top = jnp.max(logits, axis=1, keepdims=True)
    total = jnp.sum(jnp.exp(logits - top), axis=1, keepdims=True)
    lines_top, lines_total = to_lanes(top), to_lanes(total)
    if side == 1:
        other_top, other_total = before_ref[0:4, :], before_ref[4:8, :]
        best = jnp.maximum(lines_top, other_top)
        lines_total = lines_total * jnp.exp(lines_top - best) + other_total * jnp.exp(other_top - best)
        lines_top = best
    row_ref[0:4, :] = lines_top
    row_ref[4:8, :] = lines_total
    if side == 1:
        for j in range(8):
            k = (j % 4) * LANES
            part = before_sims[:, k : k + LANES] if j < 4 else sims[:, k : k + LANES]
            logits = part * tinv_ref[j : j + 1, :]
            top = jnp.max(logits, axis=0, keepdims=True)
            col_ref[j : j + 1, :] = top
            col_ref[8 + j : 9 + j, :] = jnp.sum(jnp.exp(logits - top), axis=0, keepdims=True)


def tile(side, pieces, *operands):
    operands = (*pieces, *operands)
    shapes = [
        jax.ShapeDtypeStruct((512, 512), jnp.float32),
        jax.ShapeDtypeStruct((8, LANES), jnp.float32),
    ]
    if side == 1:
        shapes += [
            jax.ShapeDtypeStruct((16, LANES), jnp.float32),
            jax.ShapeDtypeStruct((8, LANES), jnp.float32),
        ]
    return pl.pallas_call(
        functools.partial(tile_kernel, side),
        out_shape=shapes,
        in_specs=[whole()] * len(operands),
        out_specs=[whole()] * len(shapes),
        scratch_shapes=[pltpu.VMEM((512, 1024), jnp.bfloat16)] * 2,
        compiler_params=pltpu.CompilerParams(vmem_limit_bytes=24 << 20),
        cost_estimate=pl.CostEstimate(
            flops=3 << 29, bytes_accessed=6 << 20, transcendentals=1 << 19
        ),
    )(*operands)


def final_kernel(same_ref, other_ref, inv_ref, tinv_ref, row_ref, col_ref, out_ref, held, sems):
    xh = lax.axis_index("xh")
    row = from_lanes(row_ref[0:4, :] + jnp.log(row_ref[4:8, :])) - math.log(32768)
    inv = inv_ref[:, :1]
    col = col_ref[0:8, :] + jnp.log(col_ref[8:16, :]) - math.log(4096)
    copies = []
    for side, sims_ref in enumerate((same_ref, other_ref)):
        for j in range(4):
            k = 4 * side + j
            right = col[4 * side + j : 4 * side + j + 1, :]
            top = jnp.maximum(row, right)
            gap = jnp.minimum(row, right) - top
            both = top + jnp.log(1.0 + jnp.exp(gap)) - math.log(2.0)
            scale = 0.5 * (inv + tinv_ref[4 * side + j : 4 * side + j + 1, :])
            sims = sims_ref[:, j * LANES : (j + 1) * LANES]
            held[k] = sims * scale - both
            place = pl.multiple_of((2 * j + (xh ^ side)) * LANES, LANES)
            copy = pltpu.make_async_copy(held.at[k], out_ref.at[:, pl.ds(place, LANES)], sems.at[k])
            copy.start()
            copies.append(copy)
    for copy in copies:
        copy.wait()


def final(*operands):
    return pl.pallas_call(
        final_kernel,
        out_shape=jax.ShapeDtypeStruct((512, 1024), jnp.float32),
        in_specs=[whole()] * 6,
        out_specs=pl.BlockSpec(memory_space=pl.ANY),
        scratch_shapes=[pltpu.VMEM((8, 512, LANES), jnp.float32), pltpu.SemaphoreType.DMA((8,))],
        compiler_params=pltpu.CompilerParams(vmem_limit_bytes=24 << 20),
    )(*operands)


def joined(values):
    half = values[0].shape[0] // 2
    best = functools.reduce(jnp.maximum, [v[:half] for v in values])
    total = sum(v[half:] * jnp.exp(v[:half] - best) for v in values)
    return jnp.concatenate([best, total])


def gathered_rows(own):
    pair = lax.optimization_barrier(jnp.stack([own, shifted(own, "xl", 1)]))
    below = shifted(pair, "z", 2)
    above = shifted(pair, "z", -2)
    across = shifted(pair, "z", 4)
    down = shifted(jnp.concatenate([pair, below]), "z", 1)
    up = shifted(jnp.concatenate([pair, above]), "z", -1)
    near = jnp.concatenate([pair, below, above, across])
    rest = jnp.concatenate([down, up])
    return near, rest, shifted(near, "c", 1), shifted(rest, "c", 1)


def gathered_columns(tgt, inv_tgt, q, p):
    down = shifted(tgt, "y", 1)
    up = shifted(tgt, "y", -1)
    far = shifted(tgt, "y", 2)
    q = shifted(q, "xh", 1)
    q_own = shifted(p, "xh", 1)
    tail = [inv_tgt[None, :], jnp.zeros((6, LANES), jnp.float32)]
    tail = jnp.pad(jnp.concatenate(tail), ((0, 0), (0, 1024 - LANES)))
    q = jnp.concatenate([q[: REST + 1], tail])
    q_down = shifted(q, "y", 1)
    q_up = shifted(q, "y", -1)
    q_far = shifted(q, "y", 2)
    both = jnp.concatenate([down[:CUT], up[:CUT]])
    q_both = shifted(both, "xh", 1)
    q_f = shifted(far[:CUT], "xh", 1)
    same = (tgt, down, up, far)
    other = (q_own, q, q_both[:CUT], q_down, q_both[CUT:], q_up, q_f, q_far)
    return same, other, tuple(v[REST : REST + 2, :LANES] for v in (q, q_down, q_up, q_far))


def all_rows(row):
    row = joined([row, shifted(row, "c", 1)])
    row = joined([row] + [shifted(row, "z", k) for k in (2, -2, 4)])
    flip = [(i, i ^ 1) for i in range(8)]
    beside = lax.ppermute(row, "z", flip)
    crossed = lax.ppermute(
        row, ("z", "xl"), [(2 * i + k, 2 * (i ^ 1) + (k ^ 1)) for i in range(8) for k in range(2)]
    )
    return joined([row, beside, shifted(row, "xl", 1), crossed])


def all_columns(col):
    col = joined([col] + [shifted(col, "y", k) for k in (1, -1, 2)])
    over = shifted(col, "xh", 1)
    return joined([col, jnp.concatenate([over[4:8], over[0:4], over[12:16], over[8:12]])])


def body(src, inv_src, tgt, inv_tgt):
    own, q, p = first_blocks(src, inv_src, tgt, inv_tgt)
    same, other, tails = gathered_columns(tgt, inv_tgt, q, p)
    blocks = gathered_rows(own)
    hi, lo, inv = rows_ready(blocks)
    sims_same, row = tile(0, same, hi, lo, inv)
    sims_other, row, col, tinv = tile(1, other, hi, lo, inv, row, sims_same, *tails)
    col = all_columns(col)
    row = all_rows(row)
    return final(sims_same, sims_other, inv, tinv, row, col)


def solution(mesh):
    finer = Mesh(mesh.devices.reshape(4, 2, 8, 2, 2), FINE)
    placed = (P(SRC, None), P(SRC), P(TGT, None), P(TGT))
    return jax.shard_map(
        body,
        mesh=finer,
        in_specs=placed,
        out_specs=P(("y", "xh"), ("z", "xl", "c")),
        check_vma=False,
    )
```

```python
import functools
import math

import jax
import jax.numpy as jnp
from jax import lax
from jax.experimental import pallas as pl
from jax.experimental.pallas import tpu as pltpu
from jax.sharding import Mesh
from jax.sharding import PartitionSpec as P


FINE = ("y", "xh", "z", "xl", "c")
SRC = ("y", "xh", "z", "xl", "c")
TGT = ("z", "xl", "c", "y", "xh")
LANES = 128
NT = (((1,), (1,)), ((), ()))


CUT = 48
REST = LANES - CUT


def shifted(value, axis, by):
    n = lax.axis_size(axis)
    return lax.ppermute(value, axis, [(i, (i + by) % n) for i in range(n)])


def whole():
    return pl.BlockSpec(memory_space=pltpu.VMEM)


def first_kernel(src_ref, inv_ref, tgt_ref, tinv_ref, own_ref, q_ref, p_ref, rows, lane, tlane, sems):
    pairs = (
        (tgt_ref.at[CUT:], q_ref.at[:REST]),
        (tgt_ref.at[:CUT], p_ref),
        (src_ref, rows),
        (inv_ref, lane),
        (tinv_ref, tlane),
    )
    copies = [pltpu.make_async_copy(a, b, sems.at[k]) for k, (a, b) in enumerate(pairs)]
    for copy in copies:
        copy.start()
    q_ref[REST:, :] = jnp.zeros((8, 1024), jnp.float32)
    for copy in copies[2:]:
        copy.wait()
    for k in range(8):
        for r in range(2):
            at = r * 64 + k * 8
            own_ref[at : at + 8, :] = rows[r * 8 : r * 8 + 8, k * LANES : (k + 1) * LANES]
    same = lax.broadcasted_iota(jnp.int32, (16, 16), 0) == lax.broadcasted_iota(
        jnp.int32, (16, 16), 1
    )
    wide = jnp.where(same, jnp.broadcast_to(lane[...], (16, 16)), 0.0)
    own_ref[128:144, :] = jnp.broadcast_to(jnp.sum(wide, axis=1, keepdims=True), (16, LANES))
    q_ref[REST : REST + 1, :LANES] = tlane[...]
    for copy in copies[:2]:
        copy.wait()


def first_blocks(src, inv_src, tgt, inv_tgt):
    return pl.pallas_call(
        first_kernel,
        out_shape=(
            jax.ShapeDtypeStruct((144, LANES), jnp.float32),
            jax.ShapeDtypeStruct((REST + 8, 1024), jnp.float32),
            jax.ShapeDtypeStruct((CUT, 1024), jnp.float32),
        ),
        in_specs=[pl.BlockSpec(memory_space=pl.ANY)] * 4,
        out_specs=(whole(),) * 3,
        scratch_shapes=[
            pltpu.VMEM((16, 1024), jnp.float32),
            pltpu.VMEM((1, 16), jnp.float32),
            pltpu.VMEM((1, LANES), jnp.float32),
            pltpu.SemaphoreType.DMA((5,)),
        ],
        compiler_params=pltpu.CompilerParams(vmem_limit_bytes=60 << 20),
        cost_estimate=pl.CostEstimate(flops=1 << 16, bytes_accessed=1 << 20, transcendentals=0),
    )(src, inv_src[None, :], tgt, inv_tgt[None, :])


def rows_kernel(*refs):
    *groups, hi_ref, lo_ref, inv_ref = refs
    z, xl, c = lax.axis_index("z"), lax.axis_index("xl"), lax.axis_index("c")
    for (zs, dc), ref in zip(ROW_GROUPS, groups):
        at = 0
        for dz in zs:
            for dx in (0, 1):
                block = ref[at]
                at += 1
                place = lax.rem(z + dz + 8, 8) * 64 + (xl ^ dx) * 32 + (c ^ dc) * 16
                place = pl.multiple_of(place, 16)
                tiles = block[:128].reshape(2, 8, 8, LANES)
                square = jnp.sum(tiles * tiles, axis=1)
                total = jnp.sum(square, axis=-1, keepdims=True)
                scale = jnp.broadcast_to(lax.rsqrt(total + 1e-06), square.shape)
                for k in range(8):
                    unit = (tiles[:, k] * scale).reshape(16, LANES)
                    hi = unit.astype(jnp.bfloat16)
                    lo = (unit - hi.astype(jnp.float32)).astype(jnp.bfloat16)
                    hi_ref[pl.ds(place, 16), k * LANES : (k + 1) * LANES] = hi
                    lo_ref[pl.ds(place, 16), k * LANES : (k + 1) * LANES] = lo
                inv_ref[pl.ds(place, 16), :] = block[128:]


ROW_GROUPS = tuple((zs, dc) for dc in (0, 1) for zs in ((0, -2, 2, 4), (-1, -3, 1, 3)))


def rows_ready(groups):
    return pl.pallas_call(
        rows_kernel,
        out_shape=(
            jax.ShapeDtypeStruct((512, 1024), jnp.bfloat16),
            jax.ShapeDtypeStruct((512, 1024), jnp.bfloat16),
            jax.ShapeDtypeStruct((512, LANES), jnp.float32),
        ),
        in_specs=[whole()] * len(groups),
        out_specs=(whole(),) * 3,
        compiler_params=pltpu.CompilerParams(vmem_limit_bytes=16 << 20),
        cost_estimate=pl.CostEstimate(flops=8 << 20, bytes_accessed=5 << 20, transcendentals=0),
    )(*groups)


def to_lanes(column):
    same = lax.broadcasted_iota(jnp.int32, (LANES, LANES), 0) == lax.broadcasted_iota(
        jnp.int32, (LANES, LANES), 1
    )
    wide = jnp.broadcast_to(column, (512, LANES)).reshape(4, LANES, LANES)
    return jnp.sum(jnp.where(same[None], wide, 0.0), axis=1)


def from_lanes(lines):
    same = lax.broadcasted_iota(jnp.int32, (LANES, LANES), 0) == lax.broadcasted_iota(
        jnp.int32, (LANES, LANES), 1
    )
    wide = jnp.broadcast_to(lines[:, None, :], (4, LANES, LANES))
    return jnp.sum(jnp.where(same[None], wide, 0.0), axis=2).reshape(512, 1)


LAYOUTS = (((LANES,),) * 4, ((CUT, REST),) * 4)


def split_kernel(side, *refs):
    *pieces, bhi, blo = refs
    y = lax.axis_index("y")
    k = 0
    for dy, parts in zip((0, -1, 1, 2), LAYOUTS[side]):
        spot = lax.rem(y + dy + 4, 4)
        at = 0
        for rows in parts:
            value = pieces[k][:rows, :]
            k += 1
            total = jnp.sum(value * value, axis=1, keepdims=True)
            unit = value * lax.rsqrt(total + 1e-06)
            hi = unit.astype(jnp.bfloat16)
            place = pl.ds(pl.multiple_of(spot * LANES + at, 16), rows)
            bhi[place, :] = hi
            blo[place, :] = (unit - hi.astype(jnp.float32)).astype(jnp.bfloat16)
            at += rows


def split(side, pieces):
    return pl.pallas_call(
        functools.partial(split_kernel, side),
        out_shape=[jax.ShapeDtypeStruct((512, 1024), jnp.bfloat16)] * 2,
        in_specs=[whole()] * len(pieces),
        out_specs=[whole()] * 2,
        compiler_params=pltpu.CompilerParams(vmem_limit_bytes=16 << 20),
        cost_estimate=pl.CostEstimate(flops=4 << 20, bytes_accessed=4 << 20, transcendentals=0),
    )(*pieces)


def tile_kernel(side, *refs):
    if side == 1:
        n = sum(len(parts) for parts in LAYOUTS[side])
        pieces, refs = refs[:n], refs[n:]
        hi_ref, lo_ref, inv_ref, before_ref, before_sims, *refs = refs
        tails, refs = refs[:4], refs[4:]
        sims_ref, row_ref, col_ref, tinv_ref, bhi, blo = refs
        y = lax.axis_index("y")
        for dy, tail in zip((0, -1, 1, 2), tails):
            spot = lax.rem(y + dy + 4, 4)
            tinv_ref[pl.ds(spot, 1), :] = tail[1:2, :]
            tinv_ref[pl.ds(spot + 4, 1), :] = tail[0:1, :]
        split_kernel(side, *pieces, bhi, blo)
    else:
        bhi, blo, hi_ref, lo_ref, inv_ref, sims_ref, row_ref = refs
    dot = functools.partial(lax.dot_general, preferred_element_type=jnp.float32)
    sims = dot(hi_ref[...], bhi[...], NT)
    sims += dot(hi_ref[...], blo[...], NT)
    sims += dot(lo_ref[...], bhi[...], NT)
    sims_ref[...] = sims
    inv = inv_ref[:, :1]
    logits = sims * inv
    top = jnp.max(logits, axis=1, keepdims=True)
    total = jnp.sum(jnp.exp(logits - top), axis=1, keepdims=True)
    lines_top, lines_total = to_lanes(top), to_lanes(total)
    if side == 1:
        other_top, other_total = before_ref[0:4, :], before_ref[4:8, :]
        best = jnp.maximum(lines_top, other_top)
        lines_total = lines_total * jnp.exp(lines_top - best) + other_total * jnp.exp(other_top - best)
        lines_top = best
    row_ref[0:4, :] = lines_top
    row_ref[4:8, :] = lines_total
    if side == 1:
        for j in range(8):
            k = (j % 4) * LANES
            part = before_sims[:, k : k + LANES] if j < 4 else sims[:, k : k + LANES]
            logits = part * tinv_ref[j : j + 1, :]
            top = jnp.max(logits, axis=0, keepdims=True)
            col_ref[j : j + 1, :] = top
            col_ref[8 + j : 9 + j, :] = jnp.sum(jnp.exp(logits - top), axis=0, keepdims=True)


def tile(side, pieces, *operands):
    operands = (*pieces, *operands)
    shapes = [
        jax.ShapeDtypeStruct((512, 512), jnp.float32),
        jax.ShapeDtypeStruct((8, LANES), jnp.float32),
    ]
    if side == 1:
        shapes += [
            jax.ShapeDtypeStruct((16, LANES), jnp.float32),
            jax.ShapeDtypeStruct((8, LANES), jnp.float32),
        ]
    return pl.pallas_call(
        functools.partial(tile_kernel, side),
        out_shape=shapes,
        in_specs=[whole()] * len(operands),
        out_specs=[whole()] * len(shapes),
        scratch_shapes=[pltpu.VMEM((512, 1024), jnp.bfloat16)] * (2 * side),
        compiler_params=pltpu.CompilerParams(vmem_limit_bytes=24 << 20),
        cost_estimate=pl.CostEstimate(
            flops=3 << 29, bytes_accessed=6 << 20, transcendentals=1 << 19
        ),
    )(*operands)


def final_kernel(same_ref, other_ref, inv_ref, tinv_ref, row_ref, col_ref, out_ref, held, sems):
    xh = lax.axis_index("xh")
    row = from_lanes(row_ref[0:4, :] + jnp.log(row_ref[4:8, :])) - math.log(32768)
    inv = inv_ref[:, :1]
    col = col_ref[0:8, :] + jnp.log(col_ref[8:16, :]) - math.log(4096)
    copies = []
    for side, sims_ref in enumerate((same_ref, other_ref)):
        for j in range(4):
            k = 4 * side + j
            right = col[4 * side + j : 4 * side + j + 1, :]
            top = jnp.maximum(row, right)
            gap = jnp.minimum(row, right) - top
            both = top + jnp.log(1.0 + jnp.exp(gap)) - math.log(2.0)
            scale = 0.5 * (inv + tinv_ref[4 * side + j : 4 * side + j + 1, :])
            sims = sims_ref[:, j * LANES : (j + 1) * LANES]
            held[k] = sims * scale - both
            place = pl.multiple_of((2 * j + (xh ^ side)) * LANES, LANES)
            copy = pltpu.make_async_copy(held.at[k], out_ref.at[:, pl.ds(place, LANES)], sems.at[k])
            copy.start()
            copies.append(copy)
    for copy in copies:
        copy.wait()


def final(*operands):
    return pl.pallas_call(
        final_kernel,
        out_shape=jax.ShapeDtypeStruct((512, 1024), jnp.float32),
        in_specs=[whole()] * 6,
        out_specs=pl.BlockSpec(memory_space=pl.ANY),
        scratch_shapes=[pltpu.VMEM((8, 512, LANES), jnp.float32), pltpu.SemaphoreType.DMA((8,))],
        compiler_params=pltpu.CompilerParams(vmem_limit_bytes=24 << 20),
    )(*operands)


def joined(values):
    half = values[0].shape[0] // 2
    best = functools.reduce(jnp.maximum, [v[:half] for v in values])
    total = sum(v[half:] * jnp.exp(v[:half] - best) for v in values)
    return jnp.concatenate([best, total])


def gathered_rows(own):
    pair = lax.optimization_barrier(jnp.stack([own, shifted(own, "xl", 1)]))
    below = shifted(pair, "z", 2)
    above = shifted(pair, "z", -2)
    across = shifted(pair, "z", 4)
    down = shifted(jnp.concatenate([pair, below]), "z", 1)
    up = shifted(jnp.concatenate([pair, above]), "z", -1)
    near = jnp.concatenate([pair, below, above, across])
    rest = jnp.concatenate([down, up])
    return near, rest, shifted(near, "c", 1), shifted(rest, "c", 1)


def gathered_columns(tgt, inv_tgt, q, p):
    down = shifted(tgt, "y", 1)
    up = shifted(tgt, "y", -1)
    far = shifted(tgt, "y", 2)
    q = shifted(q, "xh", 1)
    q_own = shifted(p, "xh", 1)
    tail = [inv_tgt[None, :], jnp.zeros((6, LANES), jnp.float32)]
    tail = jnp.pad(jnp.concatenate(tail), ((0, 0), (0, 1024 - LANES)))
    q = jnp.concatenate([q[: REST + 1], tail])
    q_down = shifted(q, "y", 1)
    q_up = shifted(q, "y", -1)
    q_far = shifted(q, "y", 2)
    both = jnp.concatenate([down[:CUT], up[:CUT]])
    q_both = shifted(both, "xh", 1)
    q_f = shifted(far[:CUT], "xh", 1)
    same = (tgt, down, up, far)
    other = (q_own, q, q_both[:CUT], q_down, q_both[CUT:], q_up, q_f, q_far)
    return same, other, tuple(v[REST : REST + 2, :LANES] for v in (q, q_down, q_up, q_far))


def all_rows(row):
    row = joined([row, shifted(row, "c", 1)])
    steps = (2, -2, 4)
    row = joined([row] + [shifted(row, "z", k) for k in steps])
    flip = [(i, i ^ 1) for i in range(8)]
    both = [(2 * i + k, 2 * (i ^ 1) + (k ^ 1)) for i in range(8) for k in range(2)]
    beside = lax.ppermute(row, "z", flip)
    across = shifted(row, "xl", 1)
    crossed = lax.ppermute(row, ("z", "xl"), both)
    return joined([row, beside, across, crossed])


def all_columns(col):
    steps = (1, -1, 2)
    parts = [shifted(col, "y", k) for k in steps]
    col = joined([col, *parts])
    over = shifted(col, "xh", 1)
    return joined([col, jnp.concatenate([over[4:8], over[0:4], over[12:16], over[8:12]])])


def body(src, inv_src, tgt, inv_tgt):
    own, q, p = first_blocks(src, inv_src, tgt, inv_tgt)
    same, other, tails = gathered_columns(tgt, inv_tgt, q, p)
    blocks = gathered_rows(own)
    same = split(0, same)
    hi, lo, inv = rows_ready(blocks)
    sims_same, row = tile(0, same, hi, lo, inv)
    sims_other, row, col, tinv = tile(1, other, hi, lo, inv, row, sims_same, *tails)
    col = all_columns(col)
    row = all_rows(row)
    return final(sims_same, sims_other, inv, tinv, row, col)


def solution(mesh):
    finer = Mesh(mesh.devices.reshape(4, 2, 8, 2, 2), FINE)
    placed = (P(SRC, None), P(SRC), P(TGT, None), P(TGT))
    return jax.shard_map(
        body,
        mesh=finer,
        in_specs=placed,
        out_specs=P(("y", "xh"), ("z", "xl", "c")),
        check_vma=False,
    )
```

```python
import functools
import math

import jax
import jax.numpy as jnp
from jax import lax
from jax.experimental import pallas as pl
from jax.experimental.pallas import tpu as pltpu
from jax.sharding import Mesh
from jax.sharding import PartitionSpec as P


FINE = ("y", "xh", "z", "xl", "c")
SRC = ("y", "xh", "z", "xl", "c")
TGT = ("z", "xl", "c", "y", "xh")
LANES = 128
NT = (((1,), (1,)), ((), ()))


CUT = 48
REST = LANES - CUT


def shifted(value, axis, by):
    n = lax.axis_size(axis)
    return lax.ppermute(value, axis, [(i, (i + by) % n) for i in range(n)])


def whole():
    return pl.BlockSpec(memory_space=pltpu.VMEM)


def first_kernel(src_ref, inv_ref, tgt_ref, tinv_ref, own_ref, q_ref, p_ref, rows, lane, tlane, sems):
    pairs = (
        (tgt_ref.at[CUT:], q_ref.at[:REST]),
        (tgt_ref.at[:CUT], p_ref),
        (src_ref, rows),
        (inv_ref, lane),
        (tinv_ref, tlane),
    )
    copies = [pltpu.make_async_copy(a, b, sems.at[k]) for k, (a, b) in enumerate(pairs)]
    for copy in copies:
        copy.start()
    q_ref[REST:, :] = jnp.zeros((8, 1024), jnp.float32)
    for copy in copies[2:]:
        copy.wait()
    for k in range(8):
        for r in range(2):
            at = r * 64 + k * 8
            own_ref[at : at + 8, :] = rows[r * 8 : r * 8 + 8, k * LANES : (k + 1) * LANES]
    same = lax.broadcasted_iota(jnp.int32, (16, 16), 0) == lax.broadcasted_iota(
        jnp.int32, (16, 16), 1
    )
    wide = jnp.where(same, jnp.broadcast_to(lane[...], (16, 16)), 0.0)
    own_ref[128:144, :] = jnp.broadcast_to(jnp.sum(wide, axis=1, keepdims=True), (16, LANES))
    q_ref[REST : REST + 1, :LANES] = tlane[...]
    for copy in copies[:2]:
        copy.wait()


def first_blocks(src, inv_src, tgt, inv_tgt):
    return pl.pallas_call(
        first_kernel,
        out_shape=(
            jax.ShapeDtypeStruct((144, LANES), jnp.float32),
            jax.ShapeDtypeStruct((REST + 8, 1024), jnp.float32),
            jax.ShapeDtypeStruct((CUT, 1024), jnp.float32),
        ),
        in_specs=[pl.BlockSpec(memory_space=pl.ANY)] * 4,
        out_specs=(whole(),) * 3,
        scratch_shapes=[
            pltpu.VMEM((16, 1024), jnp.float32),
            pltpu.VMEM((1, 16), jnp.float32),
            pltpu.VMEM((1, LANES), jnp.float32),
            pltpu.SemaphoreType.DMA((5,)),
        ],
        compiler_params=pltpu.CompilerParams(vmem_limit_bytes=60 << 20),
        cost_estimate=pl.CostEstimate(flops=1 << 16, bytes_accessed=1 << 20, transcendentals=0),
    )(src, inv_src[None, :], tgt, inv_tgt[None, :])


def rows_kernel(*refs):
    *groups, hi_ref, lo_ref, inv_ref = refs
    z, xl, c = lax.axis_index("z"), lax.axis_index("xl"), lax.axis_index("c")
    for (zs, dc), ref in zip(ROW_GROUPS, groups):
        at = 0
        for dz in zs:
            for dx in (0, 1):
                block = ref[at]
                at += 1
                place = lax.rem(z + dz + 8, 8) * 64 + (xl ^ dx) * 32 + (c ^ dc) * 16
                place = pl.multiple_of(place, 16)
                tiles = block[:128].reshape(2, 8, 8, LANES)
                square = jnp.sum(tiles * tiles, axis=1)
                total = jnp.sum(square, axis=-1, keepdims=True)
                scale = jnp.broadcast_to(lax.rsqrt(total + 1e-06), square.shape)
                for k in range(8):
                    unit = (tiles[:, k] * scale).reshape(16, LANES)
                    hi = unit.astype(jnp.bfloat16)
                    lo = (unit - hi.astype(jnp.float32)).astype(jnp.bfloat16)
                    hi_ref[pl.ds(place, 16), k * LANES : (k + 1) * LANES] = hi
                    lo_ref[pl.ds(place, 16), k * LANES : (k + 1) * LANES] = lo
                inv_ref[pl.ds(place, 16), :] = block[128:]


ROW_GROUPS = tuple((zs, dc) for dc in (0, 1) for zs in ((0, -2, 2, 4), (-1, -3, 1, 3)))


def rows_ready(groups):
    return pl.pallas_call(
        rows_kernel,
        out_shape=(
            jax.ShapeDtypeStruct((512, 1024), jnp.bfloat16),
            jax.ShapeDtypeStruct((512, 1024), jnp.bfloat16),
            jax.ShapeDtypeStruct((512, LANES), jnp.float32),
        ),
        in_specs=[whole()] * len(groups),
        out_specs=(whole(),) * 3,
        compiler_params=pltpu.CompilerParams(vmem_limit_bytes=16 << 20),
        cost_estimate=pl.CostEstimate(flops=8 << 20, bytes_accessed=5 << 20, transcendentals=0),
    )(*groups)


def to_lanes(column):
    same = lax.broadcasted_iota(jnp.int32, (LANES, LANES), 0) == lax.broadcasted_iota(
        jnp.int32, (LANES, LANES), 1
    )
    wide = jnp.broadcast_to(column, (512, LANES)).reshape(4, LANES, LANES)
    return jnp.sum(jnp.where(same[None], wide, 0.0), axis=1)


def from_lanes(lines):
    same = lax.broadcasted_iota(jnp.int32, (LANES, LANES), 0) == lax.broadcasted_iota(
        jnp.int32, (LANES, LANES), 1
    )
    wide = jnp.broadcast_to(lines[:, None, :], (4, LANES, LANES))
    return jnp.sum(jnp.where(same[None], wide, 0.0), axis=2).reshape(512, 1)


LAYOUTS = (((LANES,),) * 4, ((CUT, REST),) * 4)


def split_kernel(side, *refs):
    *pieces, bhi, blo = refs
    y = lax.axis_index("y")
    k = 0
    for dy, parts in zip((0, -1, 1, 2), LAYOUTS[side]):
        spot = lax.rem(y + dy + 4, 4)
        at = 0
        for rows in parts:
            value = pieces[k][:rows, :]
            k += 1
            total = jnp.sum(value * value, axis=1, keepdims=True)
            unit = value * lax.rsqrt(total + 1e-06)
            hi = unit.astype(jnp.bfloat16)
            place = pl.ds(pl.multiple_of(spot * LANES + at, 16), rows)
            bhi[place, :] = hi
            blo[place, :] = (unit - hi.astype(jnp.float32)).astype(jnp.bfloat16)
            at += rows


def split(side, pieces):
    return pl.pallas_call(
        functools.partial(split_kernel, side),
        out_shape=[jax.ShapeDtypeStruct((512, 1024), jnp.bfloat16)] * 2,
        in_specs=[whole()] * len(pieces),
        out_specs=[whole()] * 2,
        compiler_params=pltpu.CompilerParams(vmem_limit_bytes=16 << 20),
        cost_estimate=pl.CostEstimate(flops=4 << 20, bytes_accessed=4 << 20, transcendentals=0),
    )(*pieces)


def tile_kernel(side, *refs):
    if side == 1:
        n = sum(len(parts) for parts in LAYOUTS[side])
        pieces, refs = refs[:n], refs[n:]
        hi_ref, lo_ref, inv_ref, before_ref, before_sims, *refs = refs
        tails, refs = refs[:4], refs[4:]
        sims_ref, row_ref, col_ref, tinv_ref, bhi, blo = refs
        y = lax.axis_index("y")
        for dy, tail in zip((0, -1, 1, 2), tails):
            spot = lax.rem(y + dy + 4, 4)
            tinv_ref[pl.ds(spot, 1), :] = tail[1:2, :]
            tinv_ref[pl.ds(spot + 4, 1), :] = tail[0:1, :]
        split_kernel(side, *pieces, bhi, blo)
    else:
        bhi, blo, hi_ref, lo_ref, inv_ref, sims_ref, row_ref = refs
    dot = functools.partial(lax.dot_general, preferred_element_type=jnp.float32)
    sims = dot(hi_ref[...], bhi[...], NT)
    sims += dot(hi_ref[...], blo[...], NT)
    sims += dot(lo_ref[...], bhi[...], NT)
    sims_ref[...] = sims
    inv = inv_ref[:, :1]
    logits = sims * inv
    top = jnp.max(logits, axis=1, keepdims=True)
    total = jnp.sum(jnp.exp(logits - top), axis=1, keepdims=True)
    lines_top, lines_total = to_lanes(top), to_lanes(total)
    if side == 1:
        other_top, other_total = before_ref[0:4, :], before_ref[4:8, :]
        best = jnp.maximum(lines_top, other_top)
        lines_total = lines_total * jnp.exp(lines_top - best) + other_total * jnp.exp(other_top - best)
        lines_top = best
    row_ref[0:4, :] = lines_top
    row_ref[4:8, :] = lines_total
    if side == 1:
        for j in range(8):
            k = (j % 4) * LANES
            part = before_sims[:, k : k + LANES] if j < 4 else sims[:, k : k + LANES]
            logits = part * tinv_ref[j : j + 1, :]
            top = jnp.max(logits, axis=0, keepdims=True)
            col_ref[j : j + 1, :] = top
            col_ref[8 + j : 9 + j, :] = jnp.sum(jnp.exp(logits - top), axis=0, keepdims=True)


def tile(side, pieces, *operands):
    operands = (*pieces, *operands)
    shapes = [
        jax.ShapeDtypeStruct((512, 512), jnp.float32),
        jax.ShapeDtypeStruct((8, LANES), jnp.float32),
    ]
    if side == 1:
        shapes += [
            jax.ShapeDtypeStruct((16, LANES), jnp.float32),
            jax.ShapeDtypeStruct((8, LANES), jnp.float32),
        ]
    return pl.pallas_call(
        functools.partial(tile_kernel, side),
        out_shape=shapes,
        in_specs=[whole()] * len(operands),
        out_specs=[whole()] * len(shapes),
        scratch_shapes=[pltpu.VMEM((512, 1024), jnp.bfloat16)] * (2 * side),
        compiler_params=pltpu.CompilerParams(vmem_limit_bytes=24 << 20),
        cost_estimate=pl.CostEstimate(
            flops=3 << 29, bytes_accessed=6 << 20, transcendentals=1 << 19
        ),
    )(*operands)


def final_kernel(same_ref, other_ref, inv_ref, tinv_ref, row_ref, col_ref, out_ref, held, sems):
    xh = lax.axis_index("xh")
    row = from_lanes(row_ref[0:4, :] + jnp.log(row_ref[4:8, :])) - math.log(32768)
    inv = inv_ref[:, :1]
    col = col_ref[0:8, :] + jnp.log(col_ref[8:16, :]) - math.log(4096)
    copies = []
    for side, sims_ref in enumerate((same_ref, other_ref)):
        for j in range(4):
            k = 4 * side + j
            right = col[4 * side + j : 4 * side + j + 1, :]
            top = jnp.maximum(row, right)
            gap = jnp.minimum(row, right) - top
            both = top + jnp.log(1.0 + jnp.exp(gap)) - math.log(2.0)
            scale = 0.5 * (inv + tinv_ref[4 * side + j : 4 * side + j + 1, :])
            sims = sims_ref[:, j * LANES : (j + 1) * LANES]
            held[k] = sims * scale - both
            place = pl.multiple_of((2 * j + (xh ^ side)) * LANES, LANES)
            copy = pltpu.make_async_copy(held.at[k], out_ref.at[:, pl.ds(place, LANES)], sems.at[k])
            copy.start()
            copies.append(copy)
    for copy in copies:
        copy.wait()


def final(*operands):
    return pl.pallas_call(
        final_kernel,
        out_shape=jax.ShapeDtypeStruct((512, 1024), jnp.float32),
        in_specs=[whole()] * 6,
        out_specs=pl.BlockSpec(memory_space=pl.ANY),
        scratch_shapes=[pltpu.VMEM((8, 512, LANES), jnp.float32), pltpu.SemaphoreType.DMA((8,))],
        compiler_params=pltpu.CompilerParams(vmem_limit_bytes=24 << 20),
    )(*operands)


def joined(values):
    half = values[0].shape[0] // 2
    best = functools.reduce(jnp.maximum, [v[:half] for v in values])
    total = sum(v[half:] * jnp.exp(v[:half] - best) for v in values)
    return jnp.concatenate([best, total])


def gathered_rows(own):
    pair = lax.optimization_barrier(jnp.stack([own, shifted(own, "xl", 1)]))
    below = shifted(pair, "z", 2)
    above = shifted(pair, "z", -2)
    across = shifted(pair, "z", 4)
    down = shifted(jnp.concatenate([pair, below]), "z", 1)
    up = shifted(jnp.concatenate([pair, above]), "z", -1)
    near = jnp.concatenate([pair, below, above, across])
    rest = jnp.concatenate([down, up])
    return near, rest, shifted(near, "c", 1), shifted(rest, "c", 1)


def gathered_columns(tgt, inv_tgt, q, p):
    down = shifted(tgt, "y", 1)
    up = shifted(tgt, "y", -1)
    far = shifted(tgt, "y", 2)
    q = shifted(q, "xh", 1)
    q_own = shifted(p, "xh", 1)
    tail = [inv_tgt[None, :], jnp.zeros((6, LANES), jnp.float32)]
    tail = jnp.pad(jnp.concatenate(tail), ((0, 0), (0, 1024 - LANES)))
    q = jnp.concatenate([q[: REST + 1], tail])
    q_down = shifted(q, "y", 1)
    q_up = shifted(q, "y", -1)
    q_far = shifted(q, "y", 2)
    both = jnp.concatenate([down[:CUT], up[:CUT]])
    q_both = shifted(both, "xh", 1)
    q_f = shifted(far[:CUT], "xh", 1)
    same = (tgt, down, up, far)
    other = (q_own, q, q_both[:CUT], q_down, q_both[CUT:], q_up, q_f, q_far)
    return same, other, tuple(v[REST : REST + 2, :LANES] for v in (q, q_down, q_up, q_far))


def all_rows(row):
    row = joined([row, shifted(row, "c", 1)])
    row = joined([row] + [shifted(row, "z", k) for k in (2, -2, 4)])
    flip = [(i, i ^ 1) for i in range(8)]
    beside = lax.ppermute(row, "z", flip)
    crossed = lax.ppermute(
        row, ("z", "xl"), [(2 * i + k, 2 * (i ^ 1) + (k ^ 1)) for i in range(8) for k in range(2)]
    )
    return joined([row, beside, shifted(row, "xl", 1), crossed])


def all_columns(col):
    col = joined([col] + [shifted(col, "y", k) for k in (1, -1, 2)])
    over = shifted(col, "xh", 1)
    return joined([col, jnp.concatenate([over[4:8], over[0:4], over[12:16], over[8:12]])])


def body(src, inv_src, tgt, inv_tgt):
    own, q, p = first_blocks(src, inv_src, tgt, inv_tgt)
    same, other, tails = gathered_columns(tgt, inv_tgt, q, p)
    blocks = gathered_rows(own)
    same = split(0, same)
    hi, lo, inv = rows_ready(blocks)
    sims_same, row = tile(0, same, hi, lo, inv)
    sims_other, row, col, tinv = tile(1, other, hi, lo, inv, row, sims_same, *tails)
    col = all_columns(col)
    row = all_rows(row)
    return final(sims_same, sims_other, inv, tinv, row, col)


def solution(mesh):
    finer = Mesh(mesh.devices.reshape(4, 2, 8, 2, 2), FINE)
    placed = (P(SRC, None), P(SRC), P(TGT, None), P(TGT))
    return jax.shard_map(
        body,
        mesh=finer,
        in_specs=placed,
        out_specs=P(("y", "xh"), ("z", "xl", "c")),
        check_vma=False,
    )
```

```python
import functools
import math

import jax
import jax.numpy as jnp
from jax import lax
from jax.experimental import pallas as pl
from jax.experimental.pallas import tpu as pltpu
from jax.sharding import Mesh
from jax.sharding import PartitionSpec as P


FINE = ("y", "xh", "z", "xl", "c")
SRC = ("y", "xh", "z", "xl", "c")
TGT = ("z", "xl", "c", "y", "xh")
LANES = 128
NT = (((1,), (1,)), ((), ()))


CUT = 48
REST = LANES - CUT


def shifted(value, axis, by):
    n = lax.axis_size(axis)
    return lax.ppermute(value, axis, [(i, (i + by) % n) for i in range(n)])


def whole():
    return pl.BlockSpec(memory_space=pltpu.VMEM)


def first_kernel(src_ref, inv_ref, tgt_ref, tinv_ref, own_ref, q_ref, p_ref, rows, lane, tlane, sems):
    pairs = (
        (tgt_ref.at[CUT:], q_ref.at[:REST]),
        (tgt_ref.at[:CUT], p_ref),
        (src_ref, rows),
        (inv_ref, lane),
        (tinv_ref, tlane),
    )
    copies = [pltpu.make_async_copy(a, b, sems.at[k]) for k, (a, b) in enumerate(pairs)]
    for copy in copies:
        copy.start()
    q_ref[REST:, :] = jnp.zeros((8, 1024), jnp.float32)
    for copy in copies[2:]:
        copy.wait()
    for k in range(8):
        for r in range(2):
            at = r * 64 + k * 8
            own_ref[at : at + 8, :] = rows[r * 8 : r * 8 + 8, k * LANES : (k + 1) * LANES]
    same = lax.broadcasted_iota(jnp.int32, (16, 16), 0) == lax.broadcasted_iota(
        jnp.int32, (16, 16), 1
    )
    wide = jnp.where(same, jnp.broadcast_to(lane[...], (16, 16)), 0.0)
    own_ref[128:144, :] = jnp.broadcast_to(jnp.sum(wide, axis=1, keepdims=True), (16, LANES))
    q_ref[REST : REST + 1, :LANES] = tlane[...]
    for copy in copies[:2]:
        copy.wait()


def first_blocks(src, inv_src, tgt, inv_tgt):
    return pl.pallas_call(
        first_kernel,
        out_shape=(
            jax.ShapeDtypeStruct((144, LANES), jnp.float32),
            jax.ShapeDtypeStruct((REST + 8, 1024), jnp.float32),
            jax.ShapeDtypeStruct((CUT, 1024), jnp.float32),
        ),
        in_specs=[pl.BlockSpec(memory_space=pl.ANY)] * 4,
        out_specs=(whole(),) * 3,
        scratch_shapes=[
            pltpu.VMEM((16, 1024), jnp.float32),
            pltpu.VMEM((1, 16), jnp.float32),
            pltpu.VMEM((1, LANES), jnp.float32),
            pltpu.SemaphoreType.DMA((5,)),
        ],
        compiler_params=pltpu.CompilerParams(vmem_limit_bytes=60 << 20),
        cost_estimate=pl.CostEstimate(flops=1 << 16, bytes_accessed=1 << 20, transcendentals=0),
    )(src, inv_src[None, :], tgt, inv_tgt[None, :])


def rows_kernel(*refs):
    *groups, hi_ref, lo_ref, inv_ref = refs
    z, xl, c = lax.axis_index("z"), lax.axis_index("xl"), lax.axis_index("c")
    for (zs, dc), ref in zip(ROW_GROUPS, groups):
        at = 0
        for dz in zs:
            for dx in (0, 1):
                block = ref[at]
                at += 1
                place = lax.rem(z + dz + 8, 8) * 64 + (xl ^ dx) * 32 + (c ^ dc) * 16
                place = pl.multiple_of(place, 16)
                tiles = block[:128].reshape(2, 8, 8, LANES)
                square = jnp.sum(tiles * tiles, axis=1)
                total = jnp.sum(square, axis=-1, keepdims=True)
                scale = jnp.broadcast_to(lax.rsqrt(total + 1e-06), square.shape)
                for k in range(8):
                    unit = (tiles[:, k] * scale).reshape(16, LANES)
                    hi = unit.astype(jnp.bfloat16)
                    lo = (unit - hi.astype(jnp.float32)).astype(jnp.bfloat16)
                    hi_ref[pl.ds(place, 16), k * LANES : (k + 1) * LANES] = hi
                    lo_ref[pl.ds(place, 16), k * LANES : (k + 1) * LANES] = lo
                inv_ref[pl.ds(place, 16), :] = block[128:]


ROW_GROUPS = tuple((zs, dc) for dc in (0, 1) for zs in ((0, -2, 2, 4), (-1, -3, 1, 3)))


def rows_ready(groups):
    return pl.pallas_call(
        rows_kernel,
        out_shape=(
            jax.ShapeDtypeStruct((512, 1024), jnp.bfloat16),
            jax.ShapeDtypeStruct((512, 1024), jnp.bfloat16),
            jax.ShapeDtypeStruct((512, LANES), jnp.float32),
        ),
        in_specs=[whole()] * len(groups),
        out_specs=(whole(),) * 3,
        compiler_params=pltpu.CompilerParams(vmem_limit_bytes=16 << 20),
        cost_estimate=pl.CostEstimate(flops=8 << 20, bytes_accessed=5 << 20, transcendentals=0),
    )(*groups)


def to_lanes(column):
    same = lax.broadcasted_iota(jnp.int32, (LANES, LANES), 0) == lax.broadcasted_iota(
        jnp.int32, (LANES, LANES), 1
    )
    wide = jnp.broadcast_to(column, (512, LANES)).reshape(4, LANES, LANES)
    return jnp.sum(jnp.where(same[None], wide, 0.0), axis=1)


def from_lanes(lines):
    same = lax.broadcasted_iota(jnp.int32, (LANES, LANES), 0) == lax.broadcasted_iota(
        jnp.int32, (LANES, LANES), 1
    )
    wide = jnp.broadcast_to(lines[:, None, :], (4, LANES, LANES))
    return jnp.sum(jnp.where(same[None], wide, 0.0), axis=2).reshape(512, 1)


LAYOUTS = (((LANES,),) * 4, ((CUT, REST),) * 4)


def split_kernel(side, *refs):
    *pieces, bhi, blo = refs
    y = lax.axis_index("y")
    k = 0
    for dy, parts in zip((0, -1, 1, 2), LAYOUTS[side]):
        spot = lax.rem(y + dy + 4, 4)
        at = 0
        for rows in parts:
            value = pieces[k][:rows, :]
            k += 1
            total = jnp.sum(value * value, axis=1, keepdims=True)
            unit = value * lax.rsqrt(total + 1e-06)
            hi = unit.astype(jnp.bfloat16)
            place = pl.ds(pl.multiple_of(spot * LANES + at, 16), rows)
            bhi[place, :] = hi
            blo[place, :] = (unit - hi.astype(jnp.float32)).astype(jnp.bfloat16)
            at += rows


def split(side, pieces):
    return pl.pallas_call(
        functools.partial(split_kernel, side),
        out_shape=[jax.ShapeDtypeStruct((512, 1024), jnp.bfloat16)] * 2,
        in_specs=[whole()] * len(pieces),
        out_specs=[whole()] * 2,
        compiler_params=pltpu.CompilerParams(vmem_limit_bytes=16 << 20),
        cost_estimate=pl.CostEstimate(flops=4 << 20, bytes_accessed=4 << 20, transcendentals=0),
    )(*pieces)


def tile_kernel(side, *refs):
    if side == 1:
        n = sum(len(parts) for parts in LAYOUTS[side])
        pieces, refs = refs[:n], refs[n:]
        hi_ref, lo_ref, inv_ref, before_ref, before_sims, *refs = refs
        tails, refs = refs[:4], refs[4:]
        sims_ref, row_ref, col_ref, tinv_ref, bhi, blo = refs
        y = lax.axis_index("y")
        for dy, tail in zip((0, -1, 1, 2), tails):
            spot = lax.rem(y + dy + 4, 4)
            tinv_ref[pl.ds(spot, 1), :] = tail[1:2, :]
            tinv_ref[pl.ds(spot + 4, 1), :] = tail[0:1, :]
        split_kernel(side, *pieces, bhi, blo)
    else:
        bhi, blo, hi_ref, lo_ref, inv_ref, sims_ref, row_ref = refs
    dot = functools.partial(lax.dot_general, preferred_element_type=jnp.float32)
    sims = dot(hi_ref[...], bhi[...], NT)
    sims += dot(hi_ref[...], blo[...], NT)
    sims += dot(lo_ref[...], bhi[...], NT)
    sims_ref[...] = sims
    inv = jnp.concatenate([inv_ref[...]] * 4, axis=1)
    logits = sims * inv
    top = jnp.max(logits, axis=1, keepdims=True)
    total = jnp.sum(jnp.exp(logits - top), axis=1, keepdims=True)
    lines_top, lines_total = to_lanes(top), to_lanes(total)
    if side == 1:
        other_top, other_total = before_ref[0:4, :], before_ref[4:8, :]
        best = jnp.maximum(lines_top, other_top)
        lines_total = lines_total * jnp.exp(lines_top - best) + other_total * jnp.exp(other_top - best)
        lines_top = best
    row_ref[0:4, :] = lines_top
    row_ref[4:8, :] = lines_total
    if side == 1:
        for j in range(8):
            k = (j % 4) * LANES
            part = before_sims[:, k : k + LANES] if j < 4 else sims[:, k : k + LANES]
            logits = part * tinv_ref[j : j + 1, :]
            top = jnp.max(logits, axis=0, keepdims=True)
            col_ref[j : j + 1, :] = top
            col_ref[8 + j : 9 + j, :] = jnp.sum(jnp.exp(logits - top), axis=0, keepdims=True)


def tile(side, pieces, *operands):
    operands = (*pieces, *operands)
    shapes = [
        jax.ShapeDtypeStruct((512, 512), jnp.float32),
        jax.ShapeDtypeStruct((8, LANES), jnp.float32),
    ]
    if side == 1:
        shapes += [
            jax.ShapeDtypeStruct((16, LANES), jnp.float32),
            jax.ShapeDtypeStruct((8, LANES), jnp.float32),
        ]
    return pl.pallas_call(
        functools.partial(tile_kernel, side),
        out_shape=shapes,
        in_specs=[whole()] * len(operands),
        out_specs=[whole()] * len(shapes),
        scratch_shapes=[pltpu.VMEM((512, 1024), jnp.bfloat16)] * (2 * side),
        compiler_params=pltpu.CompilerParams(vmem_limit_bytes=24 << 20),
        cost_estimate=pl.CostEstimate(
            flops=3 << 29, bytes_accessed=6 << 20, transcendentals=1 << 19
        ),
    )(*operands)


def final_kernel(same_ref, other_ref, inv_ref, tinv_ref, row_ref, col_ref, out_ref, held, rows, sems):
    xh = lax.axis_index("xh")
    row = from_lanes(row_ref[0:4, :] + jnp.log(row_ref[4:8, :])) - math.log(32768)
    rows[...] = jnp.broadcast_to(row, (512, LANES))
    col = col_ref[0:8, :] + jnp.log(col_ref[8:16, :]) - math.log(4096)
    copies = []
    for side, sims_ref in enumerate((same_ref, other_ref)):
        for j in range(4):
            k = 4 * side + j
            right = col[4 * side + j : 4 * side + j + 1, :]
            left = rows[...]
            top = jnp.maximum(left, right)
            gap = jnp.minimum(left, right) - top
            both = top + jnp.log(1.0 + jnp.exp(gap)) - math.log(2.0)
            scale = 0.5 * (inv_ref[...] + tinv_ref[4 * side + j : 4 * side + j + 1, :])
            sims = sims_ref[:, j * LANES : (j + 1) * LANES]
            held[k] = sims * scale - both
            place = pl.multiple_of((2 * j + (xh ^ side)) * LANES, LANES)
            copy = pltpu.make_async_copy(held.at[k], out_ref.at[:, pl.ds(place, LANES)], sems.at[k])
            copy.start()
            copies.append(copy)
    for copy in copies:
        copy.wait()


def final(*operands):
    return pl.pallas_call(
        final_kernel,
        out_shape=jax.ShapeDtypeStruct((512, 1024), jnp.float32),
        in_specs=[whole()] * 6,
        out_specs=pl.BlockSpec(memory_space=pl.ANY),
        scratch_shapes=[pltpu.VMEM((8, 512, LANES), jnp.float32), pltpu.VMEM((512, LANES), jnp.float32), pltpu.SemaphoreType.DMA((8,))],
        compiler_params=pltpu.CompilerParams(vmem_limit_bytes=24 << 20),
    )(*operands)


def joined(values):
    half = values[0].shape[0] // 2
    best = functools.reduce(jnp.maximum, [v[:half] for v in values])
    total = sum(v[half:] * jnp.exp(v[:half] - best) for v in values)
    return jnp.concatenate([best, total])


def gathered_rows(own):
    pair = lax.optimization_barrier(jnp.stack([own, shifted(own, "xl", 1)]))
    below = shifted(pair, "z", 2)
    above = shifted(pair, "z", -2)
    across = shifted(pair, "z", 4)
    down = shifted(jnp.concatenate([pair, below]), "z", 1)
    up = shifted(jnp.concatenate([pair, above]), "z", -1)
    near = jnp.concatenate([pair, below, above, across])
    rest = jnp.concatenate([down, up])
    return near, rest, shifted(near, "c", 1), shifted(rest, "c", 1)


def gathered_columns(tgt, inv_tgt, q, p):
    down = shifted(tgt, "y", 1)
    up = shifted(tgt, "y", -1)
    far = shifted(tgt, "y", 2)
    q = shifted(q, "xh", 1)
    q_own = shifted(p, "xh", 1)
    tail = [inv_tgt[None, :], jnp.zeros((6, LANES), jnp.float32)]
    tail = jnp.pad(jnp.concatenate(tail), ((0, 0), (0, 1024 - LANES)))
    q = jnp.concatenate([q[: REST + 1], tail])
    q_down = shifted(q, "y", 1)
    q_up = shifted(q, "y", -1)
    q_far = shifted(q, "y", 2)
    both = jnp.concatenate([down[:CUT], up[:CUT]])
    q_both = shifted(both, "xh", 1)
    q_f = shifted(far[:CUT], "xh", 1)
    same = (tgt, down, up, far)
    other = (q_own, q, q_both[:CUT], q_down, q_both[CUT:], q_up, q_f, q_far)
    return same, other, tuple(v[REST : REST + 2, :LANES] for v in (q, q_down, q_up, q_far))


def all_rows(row):
    row = joined([row, shifted(row, "c", 1)])
    row = joined([row] + [shifted(row, "z", k) for k in (2, -2, 4)])
    flip = [(i, i ^ 1) for i in range(8)]
    beside = lax.ppermute(row, "z", flip)
    crossed = lax.ppermute(
        row, ("z", "xl"), [(2 * i + k, 2 * (i ^ 1) + (k ^ 1)) for i in range(8) for k in range(2)]
    )
    return joined([row, beside, shifted(row, "xl", 1), crossed])


def all_columns(col):
    col = joined([col] + [shifted(col, "y", k) for k in (1, -1, 2)])
    over = shifted(col, "xh", 1)
    return joined([col, jnp.concatenate([over[4:8], over[0:4], over[12:16], over[8:12]])])


def body(src, inv_src, tgt, inv_tgt):
    own, q, p = first_blocks(src, inv_src, tgt, inv_tgt)
    same, other, tails = gathered_columns(tgt, inv_tgt, q, p)
    blocks = gathered_rows(own)
    same = split(0, same)
    hi, lo, inv = rows_ready(blocks)
    sims_same, row = tile(0, same, hi, lo, inv)
    sims_other, row, col, tinv = tile(1, other, hi, lo, inv, row, sims_same, *tails)
    col = all_columns(col)
    row = all_rows(row)
    return final(sims_same, sims_other, inv, tinv, row, col)


def solution(mesh):
    finer = Mesh(mesh.devices.reshape(4, 2, 8, 2, 2), FINE)
    placed = (P(SRC, None), P(SRC), P(TGT, None), P(TGT))
    return jax.shard_map(
        body,
        mesh=finer,
        in_specs=placed,
        out_specs=P(("y", "xh"), ("z", "xl", "c")),
        check_vma=False,
    )
```
